32 devices in a mesh: tensor: 8 (over z, core), example: 4 (over y, x).
Axes of the slice: x: 2, y: 2, z: 4, core: 2. Of those that a mesh axis runs over, the one named last changes fastest.
Arguments:
- acts: bfloat16 [256, 8192], P(None, 'example'), may hold values from -6 to 6
- out_grad: bfloat16 [256, 8192], P(None, 'example'), may hold values from -6 to 6
- w_gate: bfloat16 [8192, 28672], P('example', 'tensor'), may hold values from -0.0625 to 0.0625
- w_up: bfloat16 [8192, 28672], P('example', 'tensor'), may hold values from -0.0625 to 0.0625
- w_down: bfloat16 [28672, 8192], P('tensor', 'example'), may hold values from -0.03125 to 0.03125
- proj_in: bfloat16 [8192, 64], P('example'), may hold values from -0.0625 to 0.0625
- proj_gate: bfloat16 [28672, 64], P('tensor'), may hold values from -0.03125 to 0.03125
- proj_up: bfloat16 [28672, 64], P('tensor'), may hold values from -0.03125 to 0.03125
- proj_hidden: bfloat16 [28672, 64], P('tensor'), may hold values from -0.03125 to 0.03125
- proj_out: bfloat16 [8192, 64], P('example'), may hold values from -0.0625 to 0.0625
- store: bfloat16 [4096, 12288], P(('tensor', 'example')), may hold values from -0.0546875 to 0.0546875
- doc_ids: int32 [32, 128], P(('tensor', 'example')), may hold values from 0 to 127, each once within a row
Outputs:
- scores: float32 [4, 4096], P(None, ('tensor', 'example'))
The draws below stay inside these ranges and needn't reach their ends.
Inputs may be any that keep to these rules, and one draw needn't show every extreme that they name: Each row of doc_ids is a permutation of 0 to 127.
All inputs are finite; a program needn't handle non-finite values.
Results may differ from the reference program's by a relative error of at most 0.022.
Values may be sent and summed in bfloat16 or wider, within the bound.
No kernel may reach another device: no remote copies, remote signals or barrier semaphores. Data moves between devices by JAX's collectives and lax.ppermute only.
A program may use at most 128 MiB of HBM per device.

```python
import jax
import jax.numpy as jnp
from jax import lax

D = 8192
FF = 28672
RANK = 64
SEQ_LEN = 64
STORE_DEV = 128
TOKENS = 256
DOCS = 4096
QDIM = 12288
N_TENSOR = 8
N_EXAMPLE = 4


def raised(entries, key, source, target, blocks, factor):
    owner, partner = [(jnp.arange(entries.shape[dim]) // (entries.shape[dim] // blocks)).reshape([-1 if axis == dim else 1 for axis in range(entries.ndim)]) for dim in (source, target)]
    chosen = jax.random.permutation(key, blocks)[partner]
    strong = (owner == chosen) | (owner == (partner + blocks // 2) % blocks)
    return jnp.where(strong, factor * entries, entries)


def shard_levels(stream_key, shape, cuts, smallest, high):
    def one(dim, parts):
        steps = jax.random.uniform(jax.random.fold_in(jax.random.fold_in(stream_key, 6), dim), (parts,), jnp.float32, smallest / len(cuts), high / len(cuts))
        return jnp.repeat(jnp.exp(steps), shape[dim] // parts).reshape((-1,) + (1,) * (len(shape) - dim - 1))

    gain = one(*cuts[0])
    for cut in cuts[1:]:
        gain = gain * one(*cut)
    return gain


def gaussian(own_key, extent, spread, bound, cuts=(), held_as=jnp.bfloat16):
    gain = shard_levels(own_key, extent, cuts, -0.22, 0.18) if cuts else 1.0
    values = jax.random.normal(own_key, extent, jnp.float32) * spread * gain
    return jnp.minimum(jnp.maximum(values, -bound), bound).astype(held_as)


def heavy_noise(stream_key, extent, scale, limit, cuts, heavy, held_as=jnp.bfloat16):
    result = scale * jax.random.normal(stream_key, extent, jnp.float32)
    if cuts:
        result = result * shard_levels(stream_key, extent, cuts, -0.22, 0.18)
    return jnp.clip(raised(result, jax.random.fold_in(stream_key, 3), *heavy), -limit, limit).astype(held_as)


def setup_inputs(seed: int = 0) -> dict:
    key_of = jax.random.split(jax.random.key(seed), 13)
    return {
        "acts": heavy_noise(key_of[0], (TOKENS, D), 1.0, 6.0, ((1, 4),), (1, 0, 4, 2.0)),
        "out_grad": heavy_noise(key_of[1], (TOKENS, D), 1.0, 6.0, ((1, 4),), (1, 0, 4, 2.0)),
        "w_gate": gaussian(key_of[2], (D, FF), D ** -0.5, 0.0625, ((0, 4), (1, 8))),
        "w_up": gaussian(key_of[3], (D, FF), D ** -0.5, 0.0625, ((0, 4), (1, 8))),
        "w_down": gaussian(key_of[4], (FF, D), FF ** -0.5, 0.03125, ((0, 8), (1, 4))),
        "proj_in": gaussian(key_of[5], (D, RANK), D ** -0.5, 0.0625, ((0, 4),)),
        "proj_gate": gaussian(key_of[6], (FF, RANK), FF ** -0.5, 0.03125, ((0, 8),)),
        "proj_up": gaussian(key_of[7], (FF, RANK), FF ** -0.5, 0.03125, ((0, 8),)),
        "proj_hidden": gaussian(key_of[8], (FF, RANK), FF ** -0.5, 0.03125, ((0, 8),)),
        "proj_out": gaussian(key_of[9], (D, RANK), D ** -0.5, 0.0625, ((0, 4),)),
        "store": gaussian(key_of[10], (DOCS, QDIM), QDIM ** -0.5, 0.0546875, ((0, 32),)),
        "doc_ids": jax.vmap(lambda own: jax.random.permutation(own, STORE_DEV))(jax.random.split(key_of[11], (N_TENSOR * N_EXAMPLE))).reshape((N_TENSOR * N_EXAMPLE, STORE_DEV)).astype(jnp.int32),
    }


def grads_of(gate, up, grad_hidden):
    sig = jax.nn.sigmoid(gate)
    hidden = gate * sig * up
    grad_up = grad_hidden * gate * sig
    grad_gate = grad_hidden * up * sig * (1.0 + gate * (1.0 - sig))
    return hidden.astype(jnp.bfloat16), grad_gate.astype(jnp.bfloat16), grad_up.astype(jnp.bfloat16)


def outer_sums(left, right):
    count = left.shape[0] // SEQ_LEN
    left_seq = left.reshape(count, SEQ_LEN, left.shape[1]).astype(jnp.float32)
    right_seq = right.reshape(count, SEQ_LEN, right.shape[1]).astype(jnp.float32)
    total = jnp.einsum("stq,str->sqr", left_seq, right_seq, precision=lax.Precision.HIGHEST)
    return total.reshape(count, left.shape[1] * right.shape[1])


def width_sum(left, right, right_first):
    block = D // N_EXAMPLE
    total = None
    for index in range(N_EXAMPLE):
        left_block = left[:, index * block:(index + 1) * block]
        if right_first:
            right_block = right[index * block:(index + 1) * block, :]
            partial_term = jnp.dot(left_block, right_block, preferred_element_type=jnp.float32)
        else:
            right_block = right[:, index * block:(index + 1) * block]
            partial_term = lax.dot_general(left_block, right_block, (((1,), (1,)), ((), ())), preferred_element_type=jnp.float32)
        rounded = lax.optimization_barrier(partial_term.astype(jnp.bfloat16)).astype(jnp.float32)
        total = rounded if total is None else total + rounded
    return total


def reference(acts, out_grad, w_gate, w_up, w_down, proj_in, proj_gate, proj_up, proj_hidden, proj_out, store, doc_ids):
    gate = width_sum(acts, w_gate, True)
    up = width_sum(acts, w_up, True)
    grad_hidden = width_sum(out_grad, w_down, False)
    hidden, grad_gate, grad_up = grads_of(gate, up, grad_hidden)
    in_proj = width_sum(acts, proj_in, True)
    out_proj = width_sum(out_grad, proj_out, True)
    gate_proj = jnp.dot(grad_gate, proj_gate, preferred_element_type=jnp.float32)
    up_proj = jnp.dot(grad_up, proj_up, preferred_element_type=jnp.float32)
    hidden_proj = jnp.dot(hidden, proj_hidden, preferred_element_type=jnp.float32)
    query = jnp.concatenate([outer_sums(in_proj, gate_proj), outer_sums(in_proj, up_proj), outer_sums(hidden_proj, out_proj)], axis=1).astype(jnp.bfloat16)
    shards = doc_ids.shape[0]
    offsets = (jnp.arange(shards, dtype=jnp.int32) * STORE_DEV).astype(jnp.int32)
    rows = (doc_ids.astype(jnp.int32) + offsets[:, None]).reshape(-1).astype(jnp.int32)
    picked = jnp.take(store, rows, axis=0)
    return lax.dot_general(query, picked, (((1,), (1,)), ((), ())), preferred_element_type=jnp.float32)
```

```python
import functools

import jax
import jax.numpy as jnp
from jax import lax
from jax.experimental import pallas as pl
from jax.experimental.pallas import tpu as pltpu
from jax.sharding import PartitionSpec as P

SEQ_LEN = 64
NT = (((1,), (1,)), ((), ()))
TN = (((0,), (0,)), ((), ()))
F32 = jnp.float32
BF16 = jnp.bfloat16


def chunk_steps(total):
    if total == 14:
        return [1, 2, 3, 3, 3, 2]
    chunks, left = [1], total - 1
    while left:
        chunks.append(min(2, left))
        left -= chunks[-1]
    return chunks


def partials_kernel(count, bit, extra, width, e_ref, *refs):
    acts = jnp.concatenate([refs[j][...] for j in range(count)], axis=0)
    grads = jnp.concatenate([refs[count + j][...] for j in range(count)], axis=0)
    refs = refs[2 * count :]
    w_gate, w_up, w_down = refs[:3]
    send, keep = refs[-2:]
    parts = [
        jnp.dot(acts, w_gate[...], preferred_element_type=F32),
        jnp.dot(acts, w_up[...], preferred_element_type=F32),
        lax.dot_general(grads, w_down[...], NT, preferred_element_type=F32),
    ]
    if extra:
        parts.append(
            jnp.concatenate(
                [
                    lax.dot_general(acts, refs[3][...], NT, preferred_element_type=F32),
                    lax.dot_general(grads, refs[4][...], NT, preferred_element_type=F32),
                ],
                axis=1,
            )
        )
    at = 0
    for part in parts:
        value = part.astype(BF16)
        place = [0, 0]
        for j in range(count):
            goes = 1 if j & bit else 0
            out = send if goes else keep
            rows = pl.ds(place[goes] * SEQ_LEN, SEQ_LEN)
            out[0, rows, at : at + value.shape[1]] = value[j * SEQ_LEN : (j + 1) * SEQ_LEN]
            place[goes] += 1
        at += value.shape[1]


def partials(index, acts, grads, w_gate, w_up, w_down, extras, first, steps, width, bit):
    depth = acts.shape[1]
    count = acts.shape[0] // SEQ_LEN
    extra = len(extras) > 0
    columns = 3 * width + (2 * extras[0].shape[0] if extra else 0)
    rows = [
        pl.BlockSpec((SEQ_LEN, depth), functools.partial(lambda j, i, e: (e[0] ^ j, 0), j))
        for j in range(count)
    ]
    half = (1, count // 2 * SEQ_LEN, columns)
    shape = jax.ShapeDtypeStruct((steps,) + half[1:], BF16)
    return pl.pallas_call(
        functools.partial(partials_kernel, count, bit, extra, width),
        out_shape=(shape, shape),
        grid_spec=pltpu.PrefetchScalarGridSpec(
            num_scalar_prefetch=1,
            grid=(steps,),
            in_specs=rows
            + rows
            + [
                pl.BlockSpec((depth, width), lambda i, e: (0, first + i)),
                pl.BlockSpec((depth, width), lambda i, e: (0, first + i)),
                pl.BlockSpec((width, depth), lambda i, e: (first + i, 0)),
            ]
            + [pl.BlockSpec(x.shape, lambda i, e: (0, 0)) for x in extras],
            out_specs=[pl.BlockSpec(half, lambda i, e: (i, 0, 0))] * 2,
        ),
        compiler_params=pltpu.CompilerParams(vmem_limit_bytes=32 << 20),
        name=f"partials_{first}",
    )(index, *([acts] * count), *([grads] * count), w_gate, w_up, w_down, *extras)


def project_kernel(terms, width, *refs):
    addends, (p_gate, p_up, p_hidden, before, after) = refs[:terms], refs[terms:]
    total = functools.reduce(
        jnp.add, [ref[0, :, : 3 * width].astype(F32) for ref in addends]
    )
    gate = total[:, :width]
    up = total[:, width : 2 * width]
    back = total[:, 2 * width :]
    sig = jax.nn.sigmoid(gate)
    gs = gate * sig
    hidden = (gs * up).astype(BF16)
    grad_up = (back * gs).astype(BF16)
    grad_gate = (back * up * sig * (1.0 + gate * (1.0 - sig))).astype(BF16)
    part = jnp.concatenate(
        [
            lax.dot_general(grad_gate, p_gate[...], NT, preferred_element_type=F32),
            lax.dot_general(grad_up, p_up[...], NT, preferred_element_type=F32),
            lax.dot_general(hidden, p_hidden[...], NT, preferred_element_type=F32),
        ],
        axis=1,
    )

    @pl.when(pl.program_id(0) == 0)
    def _():
        after[...] = before[...] + part

    @pl.when(pl.program_id(0) != 0)
    def _():
        after[...] += part


def project(addends, projections, before, first, width):
    steps, _, columns = addends[0].shape
    rank = projections[0].shape[0]
    return pl.pallas_call(
        functools.partial(project_kernel, len(addends), width),
        out_shape=jax.ShapeDtypeStruct(before.shape, F32),
        grid=(steps,),
        in_specs=[pl.BlockSpec((1, SEQ_LEN, columns), lambda i: (i, 0, 0))] * len(addends)
        + [pl.BlockSpec((rank, width), lambda i: (0, first + i))] * 3
        + [pl.BlockSpec(before.shape, lambda i: (0, 0))],
        out_specs=pl.BlockSpec(before.shape, lambda i: (0, 0)),
        compiler_params=pltpu.CompilerParams(vmem_limit_bytes=16 << 20),
        name=f"project_{first}",
    )(*addends, *projections, before)


def outer_kernel(terms, at, rank, *refs):
    sums, projected, out = refs[:terms], refs[terms], refs[terms + 1]
    both = functools.reduce(jnp.add, [r[0, :, at : at + 2 * rank].astype(F32) for r in sums])
    in_proj, out_proj = both[:, :rank], both[:, rank:]
    gate_up = projected[:, : 2 * rank]
    hidden = projected[:, 2 * rank :]

    def dot(a, b):
        return lax.dot_general(
            a, b, TN, preferred_element_type=F32, precision=lax.Precision.HIGHEST
        )

    out[:, : 2 * rank] = dot(in_proj, gate_up).astype(BF16)
    out[:, 2 * rank :] = dot(hidden, out_proj).astype(BF16)


def outer(sums, projected, at, rank):
    columns = sums[0].shape[2]
    return pl.pallas_call(
        functools.partial(outer_kernel, len(sums), at, rank),
        out_shape=jax.ShapeDtypeStruct((rank, 3 * rank), BF16),
        grid=(1,),
        in_specs=[pl.BlockSpec((1, SEQ_LEN, columns), lambda i: (0, 0, 0))] * len(sums)
        + [pl.BlockSpec(projected.shape, lambda i: (0, 0))],
        out_specs=pl.BlockSpec((rank, 3 * rank), lambda i: (0, 0)),
        compiler_params=pltpu.CompilerParams(vmem_limit_bytes=16 << 20),
        name="outer",
    )(*sums, projected)


def score_kernel(count, e_ref, *refs):
    queries, (store, ids, out, rows) = refs[:count], refs[count:]
    for j in range(count):
        rows[pl.ds(e_ref[0] ^ j, 1), :] = queries[j][...].astype(F32)
    lhs = rows[...].astype(BF16)
    natural = lax.dot_general(lhs, store[...], NT, preferred_element_type=F32)
    docs = store.shape[0]
    chosen = lax.broadcasted_iota(jnp.int32, (docs, docs), 0) == ids[...]
    out[...] = jnp.dot(
        natural, chosen.astype(F32), preferred_element_type=F32, precision=lax.Precision.HIGHEST
    )


def score(index, queries, store, ids):
    count = len(queries)
    docs, size = store.shape
    vmem = pl.BlockSpec(memory_space=pltpu.VMEM)
    return pl.pallas_call(
        functools.partial(score_kernel, count),
        out_shape=jax.ShapeDtypeStruct((count, docs), F32),
        in_specs=[pl.BlockSpec(memory_space=pltpu.SMEM)] + [vmem] * (count + 2),
        out_specs=vmem,
        scratch_shapes=[pltpu.VMEM((count, size), F32)],
        compiler_params=pltpu.CompilerParams(vmem_limit_bytes=16 << 20),
        name="score",
    )(index, *queries, store, ids)


def local(
    sizes,
    acts,
    out_grad,
    w_gate,
    w_up,
    w_down,
    proj_in,
    proj_gate,
    proj_up,
    proj_hidden,
    proj_out,
    store,
    doc_ids,
):
    tensor, example = sizes
    units = w_gate.shape[1]
    rank = proj_in.shape[1]
    width = 256 if units % 256 == 0 else 128
    index = lax.axis_index("example").astype(jnp.int32).reshape(1)

    def flip(x, axis, k):
        n = tensor if axis == "tensor" else example
        return lax.ppermute(x, axis, [(i, i ^ k) for i in range(n)])

    bits = [1 << b for b in range(example.bit_length() - 1)]
    extras = (proj_in.T, proj_out.T)
    projections = (proj_gate.T, proj_up.T, proj_hidden.T)

    chunks = chunk_steps(units // width)
    ready = []
    first = 0
    for number, steps in enumerate(chunks):
        order = bits if number % 2 == 0 else bits[::-1]
        extra = extras if number == 0 else ()
        send, keep = partials(
            index, acts, out_grad, w_gate, w_up, w_down, extra, first, steps, width, order[0]
        )
        blocks = [j for j in range(example) if not j & order[0]]
        addends = [keep, flip(send, "example", order[0])]
        for bit in order[1:]:
            blocks_of = lambda x, keepers: jnp.concatenate(
                [
                    x[:, i * SEQ_LEN : (i + 1) * SEQ_LEN]
                    for i, j in enumerate(blocks)
                    if bool(j & bit) != keepers
                ],
                axis=1,
            )
            summed = lambda keepers: functools.reduce(
                jnp.add, [blocks_of(x, keepers).astype(F32) for x in addends]
            ).astype(BF16)
            send = summed(False)
            blocks = [j for j in blocks if not j & bit]
            if len(blocks) > 1:
                addends = [summed(True)]
            addends.append(flip(send, "example", bit))
        ready.append((addends, first))
        first += steps

    total = jnp.zeros((SEQ_LEN, 3 * rank), F32)
    for addends, first in ready:
        total = project(addends, projections, total, first, width)
    part = outer(ready[0][0], total, 3 * width, rank)

    pair = (part.astype(F32) + flip(part, "tensor", 1).astype(F32)).astype(BF16)
    whole = functools.reduce(
        jnp.add, [pair.astype(F32)] + [flip(pair, "tensor", k).astype(F32) for k in range(2, tensor, 2)]
    ).astype(BF16)
    query = jnp.concatenate(
        [whole[:, m * rank : (m + 1) * rank].reshape(1, rank * rank) for m in range(3)], axis=1
    )
    queries = [query] + [flip(query, "example", k) for k in range(1, example)]
    return score(index, queries, store, doc_ids)


def solution(mesh):
    return jax.shard_map(
        functools.partial(local, (mesh.shape["tensor"], mesh.shape["example"])),
        mesh=mesh,
        in_specs=(
            P(None, "example"),
            P(None, "example"),
            P("example", "tensor"),
            P("example", "tensor"),
            P("tensor", "example"),
            P("example", None),
            P("tensor", None),
            P("tensor", None),
            P("tensor", None),
            P("example", None),
            P(("tensor", "example"), None),
            P(("tensor", "example"), None),
        ),
        out_specs=P(None, ("tensor", "example")),
        check_vma=False,
    )
```

```python
import functools

import jax
import jax.numpy as jnp
from jax import lax
from jax.experimental import pallas as pl
from jax.experimental.pallas import tpu as pltpu
from jax.sharding import PartitionSpec as P

SEQ_LEN = 64
PLAN = [([], [], [(2, n % 2)]) for n in range(7)]
NT = (((1,), (1,)), ((), ()))
TN = (((0,), (0,)), ((), ()))
F32 = jnp.float32
BF16 = jnp.bfloat16


def plan_of(total):
    if total == 14:
        return PLAN
    plan = [([], [], [(1, 0)])]
    left = total - 1
    while left:
        n = len(plan)
        back = [n - 3] if n >= 3 else []
        take = [n - 5] if n >= 5 else []
        plan.append((back, take, [(min(2, left), n % 2)]))
        left -= plan[-1][2][0][0]
    return plan


def pieces_of(steps, width):
    pieces = [(2 * width * p, 2 * width) for p in range(steps // 2)]
    if steps % 2:
        pieces.append(((steps - 1) * width, width))
    return pieces


def partials_kernel(count, groups, opening, extra, first, pieces, ahead, waits, *refs):
    refs = list(refs)
    own = refs.pop(0)[0] if opening else None
    acts_in, grads_in, w_gate, w_up, w_down = refs[:5]
    refs = refs[5:]
    held = None if opening else refs.pop(0)
    p_in, p_out = (refs.pop(0), refs.pop(0)) if extra else (None, None)
    refs = refs[waits:]
    outs = [(refs.pop(0), refs.pop(0)) for _ in groups]
    acts, grads = (refs.pop(0), refs.pop(0)) if opening else (acts_in, grads_in)
    later = refs.pop(0) if ahead else None
    sems = refs.pop()
    gates = [refs.pop(0) if opening or n else held for n in range(len(pieces))]
    ups = [refs.pop(0) for _ in pieces]
    downs = [refs.pop(0) for _ in pieces]

    used = []

    def copy(source, target):
        job = pltpu.make_async_copy(source, target, sems.at[len(used)])
        job.start()
        used.append(job)
        return job

    def reorder(source, target):
        if not opening:
            return []
        return [
            copy(
                source.at[pl.ds(pl.multiple_of((own ^ j) * SEQ_LEN, SEQ_LEN), SEQ_LEN), :],
                target.at[pl.ds(j * SEQ_LEN, SEQ_LEN), :],
            )
            for j in range(count)
        ]

    wait_acts = reorder(acts_in, acts)
    wait_grads = []
    loads = []
    for number, (at, columns) in enumerate(pieces):
        hidden = pl.ds(first + at, columns)
        jobs = []
        jobs.append(copy(w_gate.at[:, hidden], gates[number]) if opening or number else None)
        jobs.append(copy(w_up.at[:, hidden], ups[number]))
        if number == 0:
            wait_grads = reorder(grads_in, grads)
        jobs.append(copy(w_down.at[hidden, :], downs[number]))
        loads.append(jobs)
    if ahead:
        at, columns = ahead
        next_load = copy(w_gate.at[:, pl.ds(at, columns)], later)

    def place(group, at, value):
        filled = [0, 0]
        for j in range(count):
            stays = 0 if j & groups[group][0] else 1
            rows = pl.ds(filled[stays] * SEQ_LEN, SEQ_LEN)
            outs[group][stays][rows, at : at + value.shape[1]] = value[
                j * SEQ_LEN : (j + 1) * SEQ_LEN
            ]
            filled[stays] += 1

    def put(kind, at, part):
        value = part.astype(BF16)
        for group, (_, begin, end) in enumerate(groups):
            low, high = max(at, begin), min(at + value.shape[1], end)
            if low < high:
                place(group, kind * (end - begin) + low - begin, value[:, low - at : high - at])

    for job in wait_acts:
        job.wait()
    for number, (at, columns) in enumerate(pieces):
        gate, up, back = loads[number]
        if gate is not None:
            gate.wait()
        put(0, at, jnp.dot(acts[...], gates[number][...], preferred_element_type=F32))
        if number == 0 and extra:
            place(
                0,
                3 * (groups[0][2] - groups[0][1]),
                jnp.concatenate(
                    [
                        lax.dot_general(acts[...], p_in[...], NT, preferred_element_type=F32),
                        lax.dot_general(grads[...], p_out[...], NT, preferred_element_type=F32),
                    ],
                    axis=1,
                ).astype(BF16),
            )
        up.wait()
        put(1, at, jnp.dot(acts[...], ups[number][...], preferred_element_type=F32))
        if number == 0:
            for job in wait_grads:
                job.wait()
        back.wait()
        put(
            2,
            at,
            lax.dot_general(grads[...], downs[number][...], NT, preferred_element_type=F32),
        )
    if ahead:
        next_load.wait()


def partials(
    own, acts, grads, w_gate, w_up, w_down, held, extras, after, first, pieces, ahead, groups, opening
):
    tokens, depth = acts.shape
    count = tokens // SEQ_LEN
    whole = sum(columns for _, columns in pieces)
    columns = 3 * whole + sum(x.shape[0] for x in extras)
    hbm = pl.BlockSpec(memory_space=pltpu.HBM)
    vmem = pl.BlockSpec(memory_space=pltpu.VMEM)
    anywhere = pl.BlockSpec(memory_space=pl.ANY)
    shapes = []
    for number, (_, begin, end) in enumerate(groups):
        own_columns = 3 * (end - begin) + (0 if number else sum(x.shape[0] for x in extras))
        shapes += [jax.ShapeDtypeStruct((count // 2 * SEQ_LEN, own_columns), BF16)] * 2
    if opening:
        shapes += [jax.ShapeDtypeStruct(acts.shape, BF16)] * 2
    if ahead:
        shapes.append(jax.ShapeDtypeStruct((depth, ahead[1]), BF16))
    rows = hbm if opening else vmem
    wide = [pltpu.VMEM((depth, c), BF16) for _, c in pieces]
    scratch = (wide if opening else wide[1:]) + wide + [
        pltpu.VMEM((c, depth), BF16) for _, c in pieces
    ]
    copies = 3 * len(pieces) + (2 * count if opening else -1) + (1 if ahead else 0)
    return pl.pallas_call(
        functools.partial(
            partials_kernel,
            count,
            groups,
            opening,
            len(extras) > 0,
            first,
            pieces,
            ahead,
            len(after),
        ),
        out_shape=shapes,
        in_specs=([pl.BlockSpec(memory_space=pltpu.SMEM)] if opening else [])
        + [rows, rows, hbm, hbm, hbm]
        + ([] if opening else [vmem])
        + [vmem] * len(extras)
        + [anywhere] * len(after),
        out_specs=[vmem] * len(shapes),
        scratch_shapes=scratch + [pltpu.SemaphoreType.DMA((copies,))],
        compiler_params=pltpu.CompilerParams(vmem_limit_bytes=32 << 20),
        cost_estimate=pl.CostEstimate(
            flops=2 * tokens * depth * columns,
            bytes_accessed=6 * depth * whole + 2 * tokens * columns,
            transcendentals=0,
        ),
        name=f"partials_{first}",
    )(
        *([own] if opening else []),
        acts,
        grads,
        w_gate,
        w_up,
        w_down,
        *([] if opening else [held]),
        *extras,
        *after,
    )


def project_kernel(terms, pieces, first, rank, sums, *refs):
    addends, refs = refs[:terms], refs[terms:]
    p_gate, p_up, p_hidden = refs[:3]
    refs = refs[3:]
    before = refs[0]
    out = refs[-1]
    whole = sum(columns for _, columns in pieces)

    def total(refs, at, columns):
        return functools.reduce(
            jnp.add, [r[:SEQ_LEN, at : at + columns].astype(F32) for r in refs]
        )

    part = before[...]
    for start, columns in pieces:
        gate = total(addends, start, columns)
        up = total(addends, whole + start, columns)
        back = total(addends, 2 * whole + start, columns)
        sig = jax.nn.sigmoid(gate)
        gs = gate * sig
        hidden = (gs * up).astype(BF16)
        grad_up = (back * gs).astype(BF16)
        grad_gate = (back * up * sig * (1.0 + gate * (1.0 - sig))).astype(BF16)
        units = slice(first + start, first + start + columns)
        part = part + jnp.concatenate(
            [
                lax.dot_general(value, weights[:, units], NT, preferred_element_type=F32)
                for value, weights in ((grad_gate, p_gate), (grad_up, p_up), (hidden, p_hidden))
            ],
            axis=1,
        )
    if sums is None:
        out[...] = part
        return
    number, at = sums
    both = total(refs[1 : 1 + number], at, 2 * rank)

    def outer(a, b):
        return lax.dot_general(
            a, b, TN, preferred_element_type=F32, precision=lax.Precision.HIGHEST
        )

    out[:, : 2 * rank] = outer(both[:, :rank], part[:, : 2 * rank]).astype(BF16)
    out[:, 2 * rank :] = outer(part[:, 2 * rank :], both[:, rank:]).astype(BF16)


def project(addends, projections, before, first, pieces, sums=(), at=0):
    rank = projections[0].shape[0]
    vmem = pl.BlockSpec(memory_space=pltpu.VMEM)
    shape = (
        jax.ShapeDtypeStruct((rank, 3 * rank), BF16)
        if sums
        else jax.ShapeDtypeStruct(before.shape, F32)
    )
    return pl.pallas_call(
        functools.partial(
            project_kernel,
            len(addends),
            pieces,
            first,
            rank,
            (len(sums), at) if sums else None,
        ),
        out_shape=shape,
        in_specs=[vmem] * (len(addends) + 4 + len(sums)),
        out_specs=vmem,
        compiler_params=pltpu.CompilerParams(vmem_limit_bytes=16 << 20),
        cost_estimate=pl.CostEstimate(
            flops=6 * SEQ_LEN * rank * sum(c for _, c in pieces),
            bytes_accessed=2 * addends[0].size,
            transcendentals=SEQ_LEN * sum(c for _, c in pieces),
        ),
        name=f"project_{first}",
    )(*addends, *projections, before, *sums)


def score_kernel(count, e_ref, *refs):
    queries, (store, ids, out, rows) = refs[:count], refs[count:]
    for j in range(count):
        rows[pl.ds(e_ref[0] ^ j, 1), :] = queries[j][...].astype(F32)
    lhs = rows[...].astype(BF16)
    natural = lax.dot_general(lhs, store[...], NT, preferred_element_type=F32)
    docs = store.shape[0]
    chosen = lax.broadcasted_iota(jnp.int32, (docs, docs), 0) == ids[...]
    out[...] = jnp.dot(
        natural, chosen.astype(F32), preferred_element_type=F32, precision=lax.Precision.HIGHEST
    )


def score(index, queries, store, ids):
    count = len(queries)
    docs, size = store.shape
    vmem = pl.BlockSpec(memory_space=pltpu.VMEM)
    return pl.pallas_call(
        functools.partial(score_kernel, count),
        out_shape=jax.ShapeDtypeStruct((count, docs), F32),
        in_specs=[pl.BlockSpec(memory_space=pltpu.SMEM)] + [vmem] * (count + 2),
        out_specs=vmem,
        scratch_shapes=[pltpu.VMEM((count, size), F32)],
        compiler_params=pltpu.CompilerParams(vmem_limit_bytes=16 << 20),
        name="score",
    )(index, *queries, store, ids)


def local(
    mesh_sizes,
    acts,
    out_grad,
    w_gate,
    w_up,
    w_down,
    proj_in,
    proj_gate,
    proj_up,
    proj_hidden,
    proj_out,
    store,
    doc_ids,
):
    tensor, example = mesh_sizes
    units = w_gate.shape[1]
    rank = proj_in.shape[1]
    width = 256 if units % 256 == 0 else 128
    index = lax.axis_index("example").astype(jnp.int32).reshape(1)

    def flip(x, axis, k):
        n = tensor if axis == "tensor" else example
        return lax.ppermute(x, axis, [(i, i ^ k) for i in range(n)])

    bits = [1 << b for b in range(example.bit_length() - 1)]
    extras = (proj_in.T, proj_out.T)
    projections = (proj_gate.T, proj_up.T, proj_hidden.T)

    def rows_of(x, blocks, chosen):
        return jnp.concatenate(
            [x[i * SEQ_LEN : (i + 1) * SEQ_LEN] for i, j in enumerate(blocks) if j in chosen],
            axis=0,
        )

    def summed(addends, blocks, chosen):
        return functools.reduce(
            jnp.add, [rows_of(x, blocks, chosen).astype(F32) for x in addends]
        ).astype(BF16)

    def later_stages(addends, order):
        blocks = [j for j in range(example) if not j & order[0]]
        sent = None
        for bit in order[1:]:
            stay = [j for j in blocks if not j & bit]
            send = summed(addends, blocks, [j for j in blocks if j & bit])
            sent = send if sent is None else sent
            if len(stay) > 1:
                addends = [summed(addends, blocks, stay)]
            addends = addends + [flip(send, "example", bit)]
            blocks = stay
        return addends, sent

    acts, out_grad, w_gate, w_up, w_down = (
        pltpu.with_memory_space_constraint(x, pltpu.HBM)
        for x in (acts, out_grad, w_gate, w_up, w_down)
    )
    plan = plan_of(units // width)
    sizes = [(steps * width, side) for _, _, call in plan for steps, side in call]
    firsts = [sum(size for size, _ in sizes[:n]) for n in range(len(sizes))]
    calls = []
    for _, _, call in plan:
        start = sum(len(c) for c in calls)
        calls.append(list(range(start, start + len(call))))
    widths = [sum(sizes[n][0] for n in call) for call in calls]
    holder = calls[min(2, len(calls) - 1)][0]
    acts_rows, grads_rows = acts, out_grad
    begun, done = [], []
    part = jnp.zeros((SEQ_LEN, 3 * rank), F32)
    sent, held, taken = None, None, 0

    def turn_back(number):
        addends, order = begun[number]
        addends, onward = later_stages(addends, order)
        done.append(addends)
        return [] if onward is None else [onward]

    def take_in(number, part):
        return project(
            done[number],
            projections,
            part,
            firsts[number],
            pieces_of(sizes[number][0] // width, width),
            *((done[holder], 3 * sizes[holder][0]) if number == len(sizes) - 1 else ()),
        )

    for index_of, (back, take, _) in enumerate(plan):
        call = calls[index_of]
        after = [] if sent is None or index_of == 0 else [sent]
        for number in back:
            after = after + turn_back(number)
        for number in take:
            part = take_in(number, part)
            after = after + [part]
            taken += 1
        first = firsts[call[0]]
        ahead = None
        if index_of + 1 < len(plan):
            ahead = (first + widths[index_of], pieces_of(widths[index_of + 1] // width, width)[0][1])
        orders = [bits[::-1] if sizes[n][1] else bits for n in call]
        results = partials(
            index,
            acts_rows,
            grads_rows,
            w_gate,
            w_up,
            w_down,
            held,
            extras if call[0] == holder else (),
            after,
            first,
            pieces_of(widths[index_of] // width, width),
            ahead,
            [
                (order[0], firsts[n] - first, firsts[n] - first + sizes[n][0])
                for n, order in zip(call, orders)
            ],
            index_of == 0,
        )
        for order in orders:
            sent, keep, *results = results
            begun.append(([keep, flip(sent, "example", order[0])], order))
        if index_of == 0:
            acts_rows, grads_rows, *results = results
        held = results[0] if ahead else None
    while len(done) < len(sizes):
        turn_back(len(done))
    while taken < len(sizes):
        part = take_in(taken, part)
        taken += 1

    pair = (part.astype(F32) + flip(part, "tensor", 1).astype(F32)).astype(BF16)
    whole = functools.reduce(
        jnp.add, [pair.astype(F32)] + [flip(pair, "tensor", k).astype(F32) for k in range(2, tensor, 2)]
    ).astype(BF16)
    query = jnp.concatenate(
        [whole[:, m * rank : (m + 1) * rank].reshape(1, rank * rank) for m in range(3)], axis=1
    )
    queries = [query] + [flip(query, "example", k) for k in range(1, example)]
    return score(index, queries, store, doc_ids)


def solution(mesh):
    return jax.shard_map(
        functools.partial(local, (mesh.shape["tensor"], mesh.shape["example"])),
        mesh=mesh,
        in_specs=(
            P(None, "example"),
            P(None, "example"),
            P("example", "tensor"),
            P("example", "tensor"),
            P("tensor", "example"),
            P("example", None),
            P("tensor", None),
            P("tensor", None),
            P("tensor", None),
            P("example", None),
            P(("tensor", "example"), None),
            P(("tensor", "example"), None),
        ),
        out_specs=P(None, ("tensor", "example")),
        check_vma=False,
    )
```

```python
import functools

import jax
import jax.numpy as jnp
from jax import lax
from jax.experimental import pallas as pl
from jax.experimental.pallas import tpu as pltpu
from jax.sharding import PartitionSpec as P

SEQ_LEN = 64
PLAN = [([], [], [(2, n % 2)]) for n in range(7)]
NT = (((1,), (1,)), ((), ()))
TN = (((0,), (0,)), ((), ()))
F32 = jnp.float32
BF16 = jnp.bfloat16


def plan_of(total):
    if total == 14:
        return PLAN
    plan = [([], [], [(1, 0)])]
    left = total - 1
    while left:
        n = len(plan)
        back = [n - 3] if n >= 3 else []
        take = [n - 5] if n >= 5 else []
        plan.append((back, take, [(min(2, left), n % 2)]))
        left -= plan[-1][2][0][0]
    return plan


def pieces_of(steps, width):
    pieces = [(2 * width * p, 2 * width) for p in range(steps // 2)]
    if steps % 2:
        pieces.append(((steps - 1) * width, width))
    return pieces


def partials_kernel(count, groups, opening, extra, first, pieces, ahead, waits, *refs):
    refs = list(refs)
    own = refs.pop(0)[0] if opening else None
    acts_in, grads_in, w_gate, w_up, w_down = refs[:5]
    refs = refs[5:]
    held = None if opening else refs.pop(0)
    p_in, p_out = (refs.pop(0), refs.pop(0)) if extra else (None, None)
    refs = refs[waits:]
    outs = [(refs.pop(0), refs.pop(0)) for _ in groups]
    acts, grads = (refs.pop(0), refs.pop(0)) if opening else (acts_in, grads_in)
    later = refs.pop(0) if ahead else None
    sems = refs.pop()
    gates = [refs.pop(0) if opening or n else held for n in range(len(pieces))]
    ups = [refs.pop(0) for _ in pieces]
    downs = [refs.pop(0) for _ in pieces]

    used = []

    def copy(source, target):
        job = pltpu.make_async_copy(source, target, sems.at[len(used)])
        job.start()
        used.append(job)
        return job

    def reorder(source, target):
        if not opening:
            return []
        return [
            copy(
                source.at[pl.ds(pl.multiple_of((own ^ j) * SEQ_LEN, SEQ_LEN), SEQ_LEN), :],
                target.at[pl.ds(j * SEQ_LEN, SEQ_LEN), :],
            )
            for j in range(count)
        ]

    wait_acts = reorder(acts_in, acts)
    wait_grads = []
    loads = []
    for number, (at, columns) in enumerate(pieces):
        hidden = pl.ds(first + at, columns)
        jobs = []
        jobs.append(copy(w_gate.at[:, hidden], gates[number]) if opening or number else None)
        jobs.append(copy(w_up.at[:, hidden], ups[number]))
        if number == 0:
            wait_grads = reorder(grads_in, grads)
        jobs.append(copy(w_down.at[hidden, :], downs[number]))
        loads.append(jobs)
    if ahead:
        at, columns = ahead
        next_load = copy(w_gate.at[:, pl.ds(at, columns)], later)

    def place(group, at, value):
        filled = [0, 0]
        for j in range(count):
            stays = 0 if j & groups[group][0] else 1
            rows = pl.ds(filled[stays] * SEQ_LEN, SEQ_LEN)
            outs[group][stays][rows, at : at + value.shape[1]] = value[
                j * SEQ_LEN : (j + 1) * SEQ_LEN
            ]
            filled[stays] += 1

    def put(kind, at, part):
        value = part.astype(BF16)
        for group, (_, begin, end) in enumerate(groups):
            low, high = max(at, begin), min(at + value.shape[1], end)
            if low < high:
                place(group, kind * (end - begin) + low - begin, value[:, low - at : high - at])

    for job in wait_acts:
        job.wait()
    for number, (at, columns) in enumerate(pieces):
        gate, up, back = loads[number]
        if gate is not None:
            gate.wait()
        put(0, at, jnp.dot(acts[...], gates[number][...], preferred_element_type=F32))
        if number == 0 and extra:
            place(
                0,
                3 * (groups[0][2] - groups[0][1]),
                jnp.concatenate(
                    [
                        lax.dot_general(acts[...], p_in[...], NT, preferred_element_type=F32),
                        lax.dot_general(grads[...], p_out[...], NT, preferred_element_type=F32),
                    ],
                    axis=1,
                ).astype(BF16),
            )
        up.wait()
        put(1, at, jnp.dot(acts[...], ups[number][...], preferred_element_type=F32))
        if number == 0:
            for job in wait_grads:
                job.wait()
        back.wait()
        put(
            2,
            at,
            lax.dot_general(grads[...], downs[number][...], NT, preferred_element_type=F32),
        )
    if ahead:
        next_load.wait()


def partials(
    own, acts, grads, w_gate, w_up, w_down, held, extras, after, first, pieces, ahead, groups, opening
):
    tokens, depth = acts.shape
    count = tokens // SEQ_LEN
    whole = sum(columns for _, columns in pieces)
    columns = 3 * whole + sum(x.shape[0] for x in extras)
    hbm = pl.BlockSpec(memory_space=pltpu.HBM)
    vmem = pl.BlockSpec(memory_space=pltpu.VMEM)
    anywhere = pl.BlockSpec(memory_space=pl.ANY)
    shapes = []
    for number, (_, begin, end) in enumerate(groups):
        own_columns = 3 * (end - begin) + (0 if number else sum(x.shape[0] for x in extras))
        shapes += [jax.ShapeDtypeStruct((count // 2 * SEQ_LEN, own_columns), BF16)] * 2
    if opening:
        shapes += [jax.ShapeDtypeStruct(acts.shape, BF16)] * 2
    if ahead:
        shapes.append(jax.ShapeDtypeStruct((depth, ahead[1]), BF16))
    rows = hbm if opening else vmem
    wide = [pltpu.VMEM((depth, c), BF16) for _, c in pieces]
    scratch = (wide if opening else wide[1:]) + wide + [
        pltpu.VMEM((c, depth), BF16) for _, c in pieces
    ]
    copies = 3 * len(pieces) + (2 * count if opening else -1) + (1 if ahead else 0)
    return pl.pallas_call(
        functools.partial(
            partials_kernel,
            count,
            groups,
            opening,
            len(extras) > 0,
            first,
            pieces,
            ahead,
            len(after),
        ),
        out_shape=shapes,
        in_specs=([pl.BlockSpec(memory_space=pltpu.SMEM)] if opening else [])
        + [rows, rows, hbm, hbm, hbm]
        + ([] if opening else [vmem])
        + [vmem] * len(extras)
        + [anywhere] * len(after),
        out_specs=[vmem] * len(shapes),
        scratch_shapes=scratch + [pltpu.SemaphoreType.DMA((copies,))],
        compiler_params=pltpu.CompilerParams(vmem_limit_bytes=32 << 20),
        cost_estimate=pl.CostEstimate(
            flops=2 * tokens * depth * columns,
            bytes_accessed=6 * depth * whole + 2 * tokens * columns,
            transcendentals=0,
        ),
        name=f"partials_{first}",
    )(
        *([own] if opening else []),
        acts,
        grads,
        w_gate,
        w_up,
        w_down,
        *([] if opening else [held]),
        *extras,
        *after,
    )


def project_kernel(terms, pieces, first, rank, sums, *refs):
    addends, refs = refs[:terms], refs[terms:]
    p_gate, p_up, p_hidden = refs[:3]
    refs = refs[3:]
    before = refs[0]
    out = refs[1 + (sums[0] if sums else 0)]
    whole = sum(columns for _, columns in pieces)

    def total(refs, at, columns):
        return functools.reduce(
            jnp.add, [r[:SEQ_LEN, at : at + columns].astype(F32) for r in refs]
        )

    part = before[...]
    for start, columns in pieces:
        gate = total(addends, start, columns)
        up = total(addends, whole + start, columns)
        back = total(addends, 2 * whole + start, columns)
        sig = jax.nn.sigmoid(gate)
        gs = gate * sig
        hidden = (gs * up).astype(BF16)
        grad_up = (back * gs).astype(BF16)
        grad_gate = (back * up * sig * (1.0 + gate * (1.0 - sig))).astype(BF16)
        units = slice(first + start, first + start + columns)
        part = part + jnp.concatenate(
            [
                lax.dot_general(value, weights[:, units], NT, preferred_element_type=F32)
                for value, weights in ((grad_gate, p_gate), (grad_up, p_up), (hidden, p_hidden))
            ],
            axis=1,
        )
    if sums is None:
        out[...] = part
        return
    number, at = sums
    both = total(refs[1 : 1 + number], at, 2 * rank)

    def outer(a, b):
        return lax.dot_general(
            a, b, TN, preferred_element_type=F32, precision=lax.Precision.HIGHEST
        )

    first_two = outer(both[:, :rank], part[:, : 2 * rank])
    products = (
        first_two[:, :rank],
        first_two[:, rank:],
        outer(part[:, 2 * rank :], both[:, rank:]),
    )
    half = rank // 2
    for number, (product, held) in enumerate(zip(products, refs[-3:])):
        held[...] = product
        pairs = [held[pl.ds(odd, half, stride=2), :] for odd in range(2)]
        out[number * half : (number + 1) * half, :] = jnp.concatenate(pairs, axis=1).astype(BF16)


def project(addends, projections, before, first, pieces, sums=(), at=0):
    rank = projections[0].shape[0]
    vmem = pl.BlockSpec(memory_space=pltpu.VMEM)
    shape = (
        jax.ShapeDtypeStruct((3 * rank // 2, 2 * rank), BF16)
        if sums
        else jax.ShapeDtypeStruct(before.shape, F32)
    )
    return pl.pallas_call(
        functools.partial(
            project_kernel,
            len(addends),
            pieces,
            first,
            rank,
            (len(sums), at) if sums else None,
        ),
        out_shape=shape,
        in_specs=[vmem] * (len(addends) + 4 + len(sums)),
        out_specs=vmem,
        scratch_shapes=[pltpu.VMEM((rank, rank), F32)] * (3 if sums else 0),
        compiler_params=pltpu.CompilerParams(vmem_limit_bytes=16 << 20),
        cost_estimate=pl.CostEstimate(
            flops=6 * SEQ_LEN * rank * sum(c for _, c in pieces),
            bytes_accessed=2 * addends[0].size,
            transcendentals=SEQ_LEN * sum(c for _, c in pieces),
        ),
        name=f"project_{first}",
    )(*addends, *projections, before, *sums)


def score_kernel(count, e_ref, *refs):
    queries, (store, ids, out, rows) = refs[:count], refs[count:]
    for j in range(count):
        query = queries[j][...].astype(F32)
        lanes = query.shape[1]
        for p in range(query.shape[0]):
            rows[j : j + 1, p * lanes : (p + 1) * lanes] = query[p : p + 1, :]
    lhs = rows[...].astype(BF16)
    natural = lax.dot_general(lhs, store[...], NT, preferred_element_type=F32)
    docs = store.shape[0]
    chosen = lax.broadcasted_iota(jnp.int32, (docs, docs), 0) == ids[...]
    scores = jnp.dot(
        natural, chosen.astype(F32), preferred_element_type=F32, precision=lax.Precision.HIGHEST
    )
    for j in range(count):
        out[pl.ds(e_ref[0] ^ j, 1), :] = scores[j : j + 1, :]


def score(index, queries, store, ids):
    count = len(queries)
    docs, size = store.shape
    vmem = pl.BlockSpec(memory_space=pltpu.VMEM)
    return pl.pallas_call(
        functools.partial(score_kernel, count),
        out_shape=jax.ShapeDtypeStruct((count, docs), F32),
        in_specs=[pl.BlockSpec(memory_space=pltpu.SMEM)] + [vmem] * (count + 2),
        out_specs=vmem,
        scratch_shapes=[pltpu.VMEM((count, size), F32)],
        compiler_params=pltpu.CompilerParams(vmem_limit_bytes=16 << 20),
        name="score",
    )(index, *queries, store, ids)


def local(
    mesh_sizes,
    acts,
    out_grad,
    w_gate,
    w_up,
    w_down,
    proj_in,
    proj_gate,
    proj_up,
    proj_hidden,
    proj_out,
    store,
    doc_ids,
):
    tensor, example = mesh_sizes
    units = w_gate.shape[1]
    rank = proj_in.shape[1]
    width = 256 if units % 256 == 0 else 128
    index = lax.axis_index("example").astype(jnp.int32).reshape(1)

    def flip(x, axis, k):
        n = tensor if axis == "tensor" else example
        return lax.ppermute(x, axis, [(i, i ^ k) for i in range(n)])

    bits = [1 << b for b in range(example.bit_length() - 1)]
    extras = (proj_in.T, proj_out.T)
    projections = (proj_gate.T, proj_up.T, proj_hidden.T)

    def rows_of(x, blocks, chosen):
        return jnp.concatenate(
            [x[i * SEQ_LEN : (i + 1) * SEQ_LEN] for i, j in enumerate(blocks) if j in chosen],
            axis=0,
        )

    def summed(addends, blocks, chosen):
        return functools.reduce(
            jnp.add, [rows_of(x, blocks, chosen).astype(F32) for x in addends]
        ).astype(BF16)

    def later_stages(addends, order):
        blocks = [j for j in range(example) if not j & order[0]]
        sent = None
        for bit in order[1:]:
            stay = [j for j in blocks if not j & bit]
            send = summed(addends, blocks, [j for j in blocks if j & bit])
            sent = send if sent is None else sent
            if len(stay) > 1:
                addends = [summed(addends, blocks, stay)]
            addends = addends + [flip(send, "example", bit)]
            blocks = stay
        return addends, sent

    acts, out_grad, w_gate, w_up, w_down = (
        pltpu.with_memory_space_constraint(x, pltpu.HBM)
        for x in (acts, out_grad, w_gate, w_up, w_down)
    )
    plan = plan_of(units // width)
    sizes = [(steps * width, side) for _, _, call in plan for steps, side in call]
    firsts = [sum(size for size, _ in sizes[:n]) for n in range(len(sizes))]
    calls = []
    for _, _, call in plan:
        start = sum(len(c) for c in calls)
        calls.append(list(range(start, start + len(call))))
    widths = [sum(sizes[n][0] for n in call) for call in calls]
    holder = calls[min(2, len(calls) - 1)][0]
    acts_rows, grads_rows = acts, out_grad
    begun, done = [], []
    part = jnp.zeros((SEQ_LEN, 3 * rank), F32)
    sent, held, taken = None, None, 0

    def turn_back(number):
        addends, order = begun[number]
        addends, onward = later_stages(addends, order)
        done.append(addends)
        return [] if onward is None else [onward]

    def take_in(number, part):
        return project(
            done[number],
            projections,
            part,
            firsts[number],
            pieces_of(sizes[number][0] // width, width),
            *((done[holder], 3 * sizes[holder][0]) if number == len(sizes) - 1 else ()),
        )

    for index_of, (back, take, _) in enumerate(plan):
        call = calls[index_of]
        after = [] if sent is None or index_of == 0 else [sent]
        for number in back:
            after = after + turn_back(number)
        for number in take:
            part = take_in(number, part)
            after = after + [part]
            taken += 1
        first = firsts[call[0]]
        ahead = None
        if index_of + 1 < len(plan):
            ahead = (first + widths[index_of], pieces_of(widths[index_of + 1] // width, width)[0][1])
        orders = [bits[::-1] if sizes[n][1] else bits for n in call]
        results = partials(
            index,
            acts_rows,
            grads_rows,
            w_gate,
            w_up,
            w_down,
            held,
            extras if call[0] == holder else (),
            after,
            first,
            pieces_of(widths[index_of] // width, width),
            ahead,
            [
                (order[0], firsts[n] - first, firsts[n] - first + sizes[n][0])
                for n, order in zip(call, orders)
            ],
            index_of == 0,
        )
        for order in orders:
            sent, keep, *results = results
            begun.append(([keep, flip(sent, "example", order[0])], order))
        if index_of == 0:
            acts_rows, grads_rows, *results = results
        held = results[0] if ahead else None
    while len(done) < len(sizes):
        turn_back(len(done))
    while taken < len(sizes):
        part = take_in(taken, part)
        taken += 1

    pair = (part.astype(F32) + flip(part, "tensor", 1).astype(F32)).astype(BF16)
    whole = functools.reduce(
        jnp.add, [pair.astype(F32)] + [flip(pair, "tensor", k).astype(F32) for k in range(2, tensor, 2)]
    ).astype(BF16)
    queries = [whole] + [flip(whole, "example", k) for k in range(1, example)]
    return score(index, queries, store, doc_ids)


def solution(mesh):
    return jax.shard_map(
        functools.partial(local, (mesh.shape["tensor"], mesh.shape["example"])),
        mesh=mesh,
        in_specs=(
            P(None, "example"),
            P(None, "example"),
            P("example", "tensor"),
            P("example", "tensor"),
            P("tensor", "example"),
            P("example", None),
            P("tensor", None),
            P("tensor", None),
            P("tensor", None),
            P("example", None),
            P(("tensor", "example"), None),
            P(("tensor", "example"), None),
        ),
        out_specs=P(None, ("tensor", "example")),
        check_vma=False,
    )
```

```python
import functools

import jax
import jax.numpy as jnp
from jax import lax
from jax.experimental import pallas as pl
from jax.experimental.pallas import tpu as pltpu
from jax.sharding import PartitionSpec as P

SEQ_LEN = 64
PLAN = [([], [], [(2, n % 2)]) for n in range(7)]
NT = (((1,), (1,)), ((), ()))
TN = (((0,), (0,)), ((), ()))
F32 = jnp.float32
BF16 = jnp.bfloat16


def plan_of(total):
    if total == 14:
        return PLAN
    plan = [([], [], [(1, 0)])]
    left = total - 1
    while left:
        n = len(plan)
        back = [n - 3] if n >= 3 else []
        take = [n - 5] if n >= 5 else []
        plan.append((back, take, [(min(2, left), n % 2)]))
        left -= plan[-1][2][0][0]
    return plan


def pieces_of(steps, width):
    pieces = [(2 * width * p, 2 * width) for p in range(steps // 2)]
    if steps % 2:
        pieces.append(((steps - 1) * width, width))
    return pieces


def partials_kernel(count, groups, opening, extra, first, pieces, ahead, waits, *refs):
    refs = list(refs)
    own = refs.pop(0)[0] if opening else None
    acts_in, grads_in, w_gate, w_up, w_down = refs[:5]
    refs = refs[5:]
    held = None if opening else refs.pop(0)
    p_in, p_out = (refs.pop(0), refs.pop(0)) if extra else (None, None)
    refs = refs[waits:]
    outs = [(refs.pop(0), refs.pop(0)) for _ in groups]
    acts, grads = (refs.pop(0), refs.pop(0)) if opening else (acts_in, grads_in)
    later = refs.pop(0) if ahead else None
    sems = refs.pop()
    gates = [refs.pop(0) if opening or n else held for n in range(len(pieces))]
    ups = [refs.pop(0) for _ in pieces]
    downs = [refs.pop(0) for _ in pieces]

    used = []

    def copy(source, target):
        job = pltpu.make_async_copy(source, target, sems.at[len(used)])
        job.start()
        used.append(job)
        return job

    def reorder(source, target):
        if not opening:
            return []
        return [
            copy(
                source.at[pl.ds(pl.multiple_of((own ^ j) * SEQ_LEN, SEQ_LEN), SEQ_LEN), :],
                target.at[pl.ds(j * SEQ_LEN, SEQ_LEN), :],
            )
            for j in range(count)
        ]

    wait_acts = reorder(acts_in, acts)
    wait_grads = []
    loads = []
    for number, (at, columns) in enumerate(pieces):
        hidden = pl.ds(first + at, columns)
        jobs = []
        jobs.append(copy(w_gate.at[:, hidden], gates[number]) if opening or number else None)
        jobs.append(copy(w_up.at[:, hidden], ups[number]))
        if number == 0:
            wait_grads = reorder(grads_in, grads)
        jobs.append(copy(w_down.at[hidden, :], downs[number]))
        loads.append(jobs)
    if ahead:
        at, columns = ahead
        next_load = copy(w_gate.at[:, pl.ds(at, columns)], later)

    def place(group, at, value):
        filled = [0, 0]
        for j in range(count):
            stays = 0 if j & groups[group][0] else 1
            rows = pl.ds(filled[stays] * SEQ_LEN, SEQ_LEN)
            outs[group][stays][rows, at : at + value.shape[1]] = value[
                j * SEQ_LEN : (j + 1) * SEQ_LEN
            ]
            filled[stays] += 1

    def put(kind, at, part):
        value = part.astype(BF16)
        for group, (_, begin, end) in enumerate(groups):
            low, high = max(at, begin), min(at + value.shape[1], end)
            if low < high:
                place(group, kind * (end - begin) + low - begin, value[:, low - at : high - at])

    for job in wait_acts:
        job.wait()
    for number, (at, columns) in enumerate(pieces):
        gate, up, back = loads[number]
        if gate is not None:
            gate.wait()
        put(0, at, jnp.dot(acts[...], gates[number][...], preferred_element_type=F32))
        if number == 0 and extra:
            place(
                0,
                3 * (groups[0][2] - groups[0][1]),
                jnp.concatenate(
                    [
                        lax.dot_general(acts[...], p_in[...], NT, preferred_element_type=F32),
                        lax.dot_general(grads[...], p_out[...], NT, preferred_element_type=F32),
                    ],
                    axis=1,
                ).astype(BF16),
            )
        up.wait()
        put(1, at, jnp.dot(acts[...], ups[number][...], preferred_element_type=F32))
        if number == 0:
            for job in wait_grads:
                job.wait()
        back.wait()
        put(
            2,
            at,
            lax.dot_general(grads[...], downs[number][...], NT, preferred_element_type=F32),
        )
    if ahead:
        next_load.wait()


def partials(
    own, acts, grads, w_gate, w_up, w_down, held, extras, after, first, pieces, ahead, groups, opening
):
    tokens, depth = acts.shape
    count = tokens // SEQ_LEN
    whole = sum(columns for _, columns in pieces)
    columns = 3 * whole + sum(x.shape[0] for x in extras)
    hbm = pl.BlockSpec(memory_space=pltpu.HBM)
    vmem = pl.BlockSpec(memory_space=pltpu.VMEM)
    anywhere = pl.BlockSpec(memory_space=pl.ANY)
    shapes = []
    for number, (_, begin, end) in enumerate(groups):
        own_columns = 3 * (end - begin) + (0 if number else sum(x.shape[0] for x in extras))
        shapes += [jax.ShapeDtypeStruct((count // 2 * SEQ_LEN, own_columns), BF16)] * 2
    if opening:
        shapes += [jax.ShapeDtypeStruct(acts.shape, BF16)] * 2
    if ahead:
        shapes.append(jax.ShapeDtypeStruct((depth, ahead[1]), BF16))
    rows = hbm if opening else vmem
    wide = [pltpu.VMEM((depth, c), BF16) for _, c in pieces]
    scratch = (wide if opening else wide[1:]) + wide + [
        pltpu.VMEM((c, depth), BF16) for _, c in pieces
    ]
    copies = 3 * len(pieces) + (2 * count if opening else -1) + (1 if ahead else 0)
    return pl.pallas_call(
        functools.partial(
            partials_kernel,
            count,
            groups,
            opening,
            len(extras) > 0,
            first,
            pieces,
            ahead,
            len(after),
        ),
        out_shape=shapes,
        in_specs=([pl.BlockSpec(memory_space=pltpu.SMEM)] if opening else [])
        + [rows, rows, hbm, hbm, hbm]
        + ([] if opening else [vmem])
        + [vmem] * len(extras)
        + [anywhere] * len(after),
        out_specs=[vmem] * len(shapes),
        scratch_shapes=scratch + [pltpu.SemaphoreType.DMA((copies,))],
        compiler_params=pltpu.CompilerParams(vmem_limit_bytes=32 << 20),
        cost_estimate=pl.CostEstimate(
            flops=2 * tokens * depth * columns,
            bytes_accessed=6 * depth * whole + 2 * tokens * columns,
            transcendentals=0,
        ),
        name=f"partials_{first}",
    )(
        *([own] if opening else []),
        acts,
        grads,
        w_gate,
        w_up,
        w_down,
        *([] if opening else [held]),
        *extras,
        *after,
    )


def project_kernel(terms, pieces, first, rank, sums, *refs):
    addends, refs = refs[:terms], refs[terms:]
    p_gate, p_up, p_hidden = refs[:3]
    refs = refs[3:]
    before = refs[0]
    out = refs[1 + (sums[0] if sums else 0)]
    whole = sum(columns for _, columns in pieces)

    def total(refs, at, columns):
        return functools.reduce(
            jnp.add, [r[:SEQ_LEN, at : at + columns].astype(F32) for r in refs]
        )

    part = before[...]
    for start, columns in pieces:
        gate = total(addends, start, columns)
        up = total(addends, whole + start, columns)
        back = total(addends, 2 * whole + start, columns)
        sig = jax.nn.sigmoid(gate)
        gs = gate * sig
        hidden = (gs * up).astype(BF16)
        grad_up = (back * gs).astype(BF16)
        grad_gate = (back * up * sig * (1.0 + gate * (1.0 - sig))).astype(BF16)
        units = slice(first + start, first + start + columns)
        part = part + jnp.concatenate(
            [
                lax.dot_general(value, weights[:, units], NT, preferred_element_type=F32)
                for value, weights in ((grad_gate, p_gate), (grad_up, p_up), (hidden, p_hidden))
            ],
            axis=1,
        )
    if sums is None:
        out[...] = part
        return
    number, at = sums
    both = total(refs[1 : 1 + number], at, 2 * rank)

    def outer(a, b):
        return lax.dot_general(
            a, b, TN, preferred_element_type=F32, precision=lax.Precision.HIGHEST
        )

    first_two = outer(both[:, :rank], part[:, : 2 * rank])
    products = (
        first_two[:, :rank],
        first_two[:, rank:],
        outer(part[:, 2 * rank :], both[:, rank:]),
    )
    half = rank // 2
    for number, (product, held) in enumerate(zip(products, refs[-3:])):
        held[...] = product
        pairs = [held[pl.ds(odd, half, stride=2), :] for odd in range(2)]
        out[number * half : (number + 1) * half, :] = jnp.concatenate(pairs, axis=1).astype(BF16)


def project(addends, projections, before, first, pieces, sums=(), at=0):
    rank = projections[0].shape[0]
    vmem = pl.BlockSpec(memory_space=pltpu.VMEM)
    shape = (
        jax.ShapeDtypeStruct((3 * rank // 2, 2 * rank), BF16)
        if sums
        else jax.ShapeDtypeStruct(before.shape, F32)
    )
    return pl.pallas_call(
        functools.partial(
            project_kernel,
            len(addends),
            pieces,
            first,
            rank,
            (len(sums), at) if sums else None,
        ),
        out_shape=shape,
        in_specs=[vmem] * (len(addends) + 4 + len(sums)),
        out_specs=vmem,
        scratch_shapes=[pltpu.VMEM((rank, rank), F32)] * (3 if sums else 0),
        compiler_params=pltpu.CompilerParams(vmem_limit_bytes=16 << 20),
        cost_estimate=pl.CostEstimate(
            flops=6 * SEQ_LEN * rank * sum(c for _, c in pieces),
            bytes_accessed=2 * addends[0].size,
            transcendentals=SEQ_LEN * sum(c for _, c in pieces),
        ),
        name=f"project_{first}",
    )(*addends, *projections, before, *sums)


def score_kernel(count, e_ref, *refs):
    queries, (store, ids, out, rows) = refs[:count], refs[count:]
    for j in range(count):
        query = queries[j][...].astype(F32)
        lanes = query.shape[1]
        for p in range(query.shape[0]):
            rows[j : j + 1, p * lanes : (p + 1) * lanes] = query[p : p + 1, :]
    lhs = rows[...].astype(BF16)
    natural = lax.dot_general(lhs, store[...], NT, preferred_element_type=F32)
    docs = store.shape[0]
    chosen = lax.broadcasted_iota(jnp.int32, (docs, docs), 0) == ids[...]
    scores = jnp.dot(
        natural, chosen.astype(F32), preferred_element_type=F32, precision=lax.Precision.HIGHEST
    )
    for j in range(count):
        out[pl.ds(e_ref[0] ^ j, 1), :] = scores[j : j + 1, :]


def score(index, queries, store, ids):
    count = len(queries)
    docs, size = store.shape
    vmem = pl.BlockSpec(memory_space=pltpu.VMEM)
    return pl.pallas_call(
        functools.partial(score_kernel, count),
        out_shape=jax.ShapeDtypeStruct((count, docs), F32),
        in_specs=[pl.BlockSpec(memory_space=pltpu.SMEM)] + [vmem] * (count + 2),
        out_specs=vmem,
        scratch_shapes=[pltpu.VMEM((count, size), F32)],
        compiler_params=pltpu.CompilerParams(vmem_limit_bytes=16 << 20),
        name="score",
    )(index, *queries, store, ids)


def local(
    mesh_sizes,
    acts,
    out_grad,
    w_gate,
    w_up,
    w_down,
    proj_in,
    proj_gate,
    proj_up,
    proj_hidden,
    proj_out,
    store,
    doc_ids,
):
    tensor, example = mesh_sizes
    units = w_gate.shape[1]
    rank = proj_in.shape[1]
    width = 256 if units % 256 == 0 else 128
    index = lax.axis_index("example").astype(jnp.int32).reshape(1)

    def flip(x, axis, k):
        n = tensor if axis == "tensor" else example
        return lax.ppermute(x, axis, [(i, i ^ k) for i in range(n)])

    bits = [1 << b for b in range(example.bit_length() - 1)]
    extras = (proj_in.T, proj_out.T)
    projections = (proj_gate.T, proj_up.T, proj_hidden.T)

    def rows_of(x, blocks, chosen):
        return jnp.concatenate(
            [x[i * SEQ_LEN : (i + 1) * SEQ_LEN] for i, j in enumerate(blocks) if j in chosen],
            axis=0,
        )

    def summed(addends, blocks, chosen):
        return functools.reduce(
            jnp.add, [rows_of(x, blocks, chosen).astype(F32) for x in addends]
        ).astype(BF16)

    def later_stages(addends, order):
        blocks = [j for j in range(example) if not j & order[0]]
        sent = None
        for bit in order[1:]:
            stay = [j for j in blocks if not j & bit]
            send = summed(addends, blocks, [j for j in blocks if j & bit])
            sent = send if sent is None else sent
            if len(stay) > 1:
                addends = [summed(addends, blocks, stay)]
            addends = addends + [flip(send, "example", bit)]
            blocks = stay
        return addends, sent

    acts, out_grad, w_gate, w_up, w_down = (
        pltpu.with_memory_space_constraint(x, pltpu.HBM)
        for x in (acts, out_grad, w_gate, w_up, w_down)
    )
    plan = plan_of(units // width)
    sizes = [(steps * width, side) for _, _, call in plan for steps, side in call]
    firsts = [sum(size for size, _ in sizes[:n]) for n in range(len(sizes))]
    calls = []
    for _, _, call in plan:
        start = sum(len(c) for c in calls)
        calls.append(list(range(start, start + len(call))))
    widths = [sum(sizes[n][0] for n in call) for call in calls]
    holder = calls[min(4, len(calls) - 1)][0]
    acts_rows, grads_rows = acts, out_grad
    begun, done = [], []
    part = jnp.zeros((SEQ_LEN, 3 * rank), F32)
    sent, held, taken = None, None, 0

    def turn_back(number):
        addends, order = begun[number]
        addends, onward = later_stages(addends, order)
        done.append(addends)
        return [] if onward is None else [onward]

    def take_in(number, part):
        return project(
            done[number],
            projections,
            part,
            firsts[number],
            pieces_of(sizes[number][0] // width, width),
            *((done[holder], 3 * sizes[holder][0]) if number == len(sizes) - 1 else ()),
        )

    for index_of, (back, take, _) in enumerate(plan):
        call = calls[index_of]
        after = [] if sent is None or index_of == 0 else [sent]
        for number in back:
            after = after + turn_back(number)
        for number in take:
            part = take_in(number, part)
            after = after + [part]
            taken += 1
        first = firsts[call[0]]
        ahead = None
        if index_of + 1 < len(plan):
            ahead = (first + widths[index_of], pieces_of(widths[index_of + 1] // width, width)[0][1])
        orders = [bits[::-1] if sizes[n][1] else bits for n in call]
        results = partials(
            index,
            acts_rows,
            grads_rows,
            w_gate,
            w_up,
            w_down,
            held,
            extras if call[0] == holder else (),
            after,
            first,
            pieces_of(widths[index_of] // width, width),
            ahead,
            [
                (order[0], firsts[n] - first, firsts[n] - first + sizes[n][0])
                for n, order in zip(call, orders)
            ],
            index_of == 0,
        )
        for order in orders:
            sent, keep, *results = results
            begun.append(([keep, flip(sent, "example", order[0])], order))
        if index_of == 0:
            acts_rows, grads_rows, *results = results
        held = results[0] if ahead else None
    while len(done) < len(sizes):
        turn_back(len(done))
    while taken < len(sizes):
        part = take_in(taken, part)
        taken += 1

    pair = (part.astype(F32) + flip(part, "tensor", 1).astype(F32)).astype(BF16)
    whole = functools.reduce(
        jnp.add, [pair.astype(F32)] + [flip(pair, "tensor", k).astype(F32) for k in range(2, tensor, 2)]
    ).astype(BF16)
    queries = [whole] + [flip(whole, "example", k) for k in range(1, example)]
    return score(index, queries, store, doc_ids)


def solution(mesh):
    return jax.shard_map(
        functools.partial(local, (mesh.shape["tensor"], mesh.shape["example"])),
        mesh=mesh,
        in_specs=(
            P(None, "example"),
            P(None, "example"),
            P("example", "tensor"),
            P("example", "tensor"),
            P("tensor", "example"),
            P("example", None),
            P("tensor", None),
            P("tensor", None),
            P("tensor", None),
            P("example", None),
            P(("tensor", "example"), None),
            P(("tensor", "example"), None),
        ),
        out_specs=P(None, ("tensor", "example")),
        check_vma=False,
    )
```
